512 devices in a mesh: uv: 64 (over z, y), freq: 8 (over x, core).
Axes of the slice: x: 4, y: 4, z: 16, core: 2. Of those that a mesh axis runs over, the one named last changes fastest.
Arguments:
- model_image: bfloat16 [2048, 2048], P('uv'), may hold values from -6 to 6
- visibilities: float32 [2, 64, 8, 64, 32], P(None, 'uv', 'freq'), may hold values from -6 to 6
- cell_rows: int32 [64, 8, 64, 32], P('uv', 'freq'), may hold values from 0 to 31
- cell_cols: int32 [64, 8, 64, 32], P('uv', 'freq'), may hold values from 0 to 2047
- kernel_offsets: int32 [2, 64, 8, 64, 32], P(None, 'uv', 'freq'), may hold values from 0 to 127
- slot_counts: int32 [64, 8, 64], P('uv', 'freq'), may hold values from 1 to 32, as said below
- kernel_table: float32 [128, 8], replicated, may hold values from 0.05 to 1
Outputs:
- residual_vis: float32 [2, 64, 8, 64, 32], P(None, 'uv', 'freq')
- gradient: float32 [2048, 2048], P('uv', 'freq')
The draws below stay inside these ranges and needn't reach their ends.
Inputs may be any that keep to these rules, and one draw needn't show every extreme that they name: Slots 0 .. slot_counts - 1 of a sender tile, group and destination tile are live; in every draw some destination tile receives 32 live slots from every sender tile of every group.
All inputs are finite; a program needn't handle non-finite values.
Results may differ from the reference program's by a relative error of at most 0.013.
Values may be sent and summed in bfloat16 or wider, within the bound.
A program may use at most 64 MiB of HBM per device.

```python
import jax
import jax.numpy as jnp
from jax import lax

FACET = 2048
TAPS = 8
OVER = 128
CAP = 32
TILES = 64
GROUPS = 8
STRIP = 32


def draw_slot_counts(key, part):
    center_key, base_key = jax.random.split(key)
    center = jax.random.randint(center_key, (), 0, TILES)
    destination = jnp.arange(TILES, dtype=jnp.int32)
    distance = jnp.abs(destination - center)
    distance = jnp.minimum(distance, TILES - distance)
    level = jnp.maximum(1, 4 - distance * 8 // TILES)
    base_counts = jax.random.randint(base_key, (TILES, GROUPS, TILES), 0, CAP)
    counts = 1 + base_counts * (level + 4)[None, None, :] // 8
    return jnp.where((destination == center)[None, None, :], CAP, counts).astype(jnp.int32)


def plant(values, key, smallest, largest):
    longest = values.shape.index(max(values.shape))
    spots = []
    for shift in (0, 1):
        where = [jax.random.randint(jax.random.fold_in(key, axis), (), 0, length) for axis, length in enumerate(values.shape)]
        where[longest] = (where[longest] + shift) % values.shape[longest]
        spots.append(tuple(where))
    return values.at[spots[0]].set(smallest).at[spots[1]].set(largest)


def block_levels(stream_key, extent, shards, smallest, largest):
    def one(axis_at, blocks):
        steps = jax.random.uniform(jax.random.fold_in(jax.random.fold_in(stream_key, 6), axis_at), (blocks,), jnp.float32, smallest / len(shards), largest / len(shards))
        return jnp.repeat(jnp.exp(steps), extent[axis_at] // blocks).reshape((-1,) + (1,) * (len(extent) - axis_at - 1))

    level = one(*shards[0])
    for cut in shards[1:]:
        level = level * one(*cut)
    return level


def noise(own_key, extent, deviation, limit, cuts=(), kind=jnp.bfloat16):
    result = deviation * jax.random.normal(own_key, extent, jnp.float32)
    if cuts:
        result = result * block_levels(own_key, extent, cuts, -0.22, 0.18)
    return jnp.clip(result, -limit, limit).astype(kind)


def setup_inputs(seed: int = 0) -> dict:
    keys = jax.random.split(jax.random.key(seed), 8)
    model_image = noise(keys[0], (FACET, FACET), 1.0, 6.0, ((0, 64),))
    visibilities = noise(keys[1], (2, TILES, GROUPS, TILES, CAP), 1.0, 6.0, ((1, 64), (2, 8)), jnp.float32)
    cell_rows = plant(jax.random.randint(keys[2], (TILES, GROUPS, TILES, CAP), 0, STRIP), jax.random.fold_in(keys[2], 1), 0, STRIP - 1).astype(jnp.int32)
    cell_cols = plant(jax.random.randint(keys[3], (TILES, GROUPS, TILES, CAP), 0, FACET), jax.random.fold_in(keys[3], 1), 0, FACET - 1).astype(jnp.int32)
    kernel_offsets = plant(jax.random.randint(keys[4], (2, TILES, GROUPS, TILES, CAP), 0, OVER), jax.random.fold_in(keys[4], 1), 0, OVER - 1).astype(jnp.int32)
    slot_counts = draw_slot_counts(jax.random.fold_in(keys[7], 71), 0)
    kernel_table = jnp.clip(jax.random.uniform(keys[6], (OVER, TAPS), jnp.float32, 0.05, 1.0), 0.05, 1.0)
    return {"model_image": model_image, "visibilities": visibilities, "cell_rows": cell_rows, "cell_cols": cell_cols, "kernel_offsets": kernel_offsets, "slot_counts": slot_counts, "kernel_table": kernel_table}


def round_pair(complex_values):
    real_part = lax.optimization_barrier(jnp.real(complex_values).astype(jnp.bfloat16)).astype(jnp.float32)
    imaginary_part = lax.optimization_barrier(jnp.imag(complex_values).astype(jnp.bfloat16)).astype(jnp.float32)
    return real_part, imaginary_part


def reference(model_image, visibilities, cell_rows, cell_cols, kernel_offsets, slot_counts, kernel_table):
    facet_width = FACET
    strip_rows = FACET // TILES
    image_values = model_image.astype(jnp.float32)
    half_real, half_imaginary = round_pair(jnp.fft.fft(image_values, axis=1))
    grid_complex = jnp.fft.fft(lax.complex(half_real, half_imaginary), axis=0).T / facet_width
    grid_real, grid_imaginary = round_pair(grid_complex)
    tap_range = jnp.arange(TAPS, dtype=jnp.int32)
    factors_u = kernel_table[kernel_offsets[0]]
    narrow_v = lax.optimization_barrier(kernel_table[kernel_offsets[1]].astype(jnp.bfloat16)).astype(jnp.float32)
    tile_start = (jnp.arange(TILES, dtype=jnp.int32) * strip_rows)[None, None, :, None]
    row_index = ((tile_start + cell_rows)[..., None] + tap_range) % facet_width
    col_index = (cell_cols[..., None] + tap_range) % facet_width
    live_slots = (jnp.arange(CAP, dtype=jnp.int32)[None, None, None, :] < slot_counts[..., None]).astype(jnp.float32)

    def one_group(group_inputs):
        vis_group, rows_group, cols_group, factor_rows, factor_cols, live_group = group_inputs
        rows_full = jnp.broadcast_to(rows_group[..., :, None], rows_group.shape + (TAPS,))
        cols_full = jnp.broadcast_to(cols_group[..., None, :], cols_group.shape[:-1] + (TAPS, TAPS))
        weights = factor_rows[..., :, None] * factor_cols[..., None, :]
        model_real = jnp.sum(weights * grid_real[rows_full, cols_full], axis=(-2, -1))
        model_imaginary = jnp.sum(weights * grid_imaginary[rows_full, cols_full], axis=(-2, -1))
        residual_real = live_group * (vis_group[0] - model_real)
        residual_imaginary = live_group * (vis_group[1] - model_imaginary)
        deposit_real = lax.optimization_barrier((factor_rows * residual_real[..., None]).astype(jnp.bfloat16)).astype(jnp.float32)
        deposit_imaginary = lax.optimization_barrier((factor_rows * residual_imaginary[..., None]).astype(jnp.bfloat16)).astype(jnp.float32)
        spread_real = deposit_real[..., :, None] * factor_cols[..., None, :]
        spread_imaginary = deposit_imaginary[..., :, None] * factor_cols[..., None, :]
        empty_grid = jnp.zeros((facet_width, facet_width), jnp.float32)
        grid_residual_real = empty_grid.at[rows_full, cols_full].add(spread_real)
        grid_residual_imaginary = empty_grid.at[rows_full, cols_full].add(spread_imaginary)
        half_grid = jnp.fft.ifft(lax.complex(grid_residual_real, grid_residual_imaginary), axis=1) * facet_width
        half_grid_real, half_grid_imaginary = round_pair(half_grid)
        dirty_image = jnp.real(jnp.fft.ifft(lax.complex(half_grid_real, half_grid_imaginary), axis=0)).T
        return dirty_image, jnp.stack([residual_real, residual_imaginary])

    group_inputs = (jnp.moveaxis(visibilities, 2, 0), jnp.moveaxis(row_index, 1, 0), jnp.moveaxis(col_index, 1, 0),
                    jnp.moveaxis(factors_u, 1, 0), jnp.moveaxis(narrow_v, 1, 0), jnp.moveaxis(live_slots, 1, 0))
    dirty_all, residual_all = lax.map(one_group, group_inputs)
    gradient = jnp.sum(dirty_all, axis=0)
    residual_vis = jnp.moveaxis(residual_all, 0, 2)
    return residual_vis, gradient
```

```python
import functools

import jax
import jax.numpy as jnp
import numpy as np
from jax import lax
from jax.experimental import pallas as pl
from jax.experimental.pallas import tpu as pltpu
from jax.sharding import PartitionSpec as P

MESH = pl.DeviceIdType.MESH
WIDTH = 2048
TILES = 64
GROUPS = 8
STRIP = 32
OWN = 5
SLOTS = 32
TAPS = 8
BLOCKS = 16
ROWS = GROUPS * OWN * 2 * BLOCKS
PIECE = OWN * 2 * BLOCKS
BATCH = 256
F32 = jnp.float32
BF16 = jnp.bfloat16


def tables():
    turn = 2.0 * np.pi
    v = np.arange(TILES)[:, None]
    m = np.arange(128)[None, :]
    coarse = np.stack([np.cos(turn * (v * m % 64) / 64), np.sin(turn * (v * m % 64) / 64)])
    rows = np.arange(GROUPS * OWN)[:, None] * np.arange(WIDTH)[None, :] % WIDTH
    fine = np.zeros((GROUPS, 16, WIDTH))
    fine[:, 0:OWN] = np.cos(turn * rows / WIDTH).reshape(GROUPS, OWN, WIDTH)
    fine[:, 8 : 8 + OWN] = np.sin(turn * rows / WIDTH).reshape(GROUPS, OWN, WIDTH)
    q1 = np.arange(64)[:, None]
    u = np.arange(64)[None, :]
    cos64, sin64 = np.cos(turn * (q1 * u % 64) / 64), np.sin(turn * (q1 * u % 64) / 64)
    outer = np.block([[cos64, sin64], [-sin64, cos64]])
    l0 = np.arange(STRIP)
    twist = np.zeros((2, 64, 256))
    twist[0, :, : OWN * STRIP] = np.tile(np.cos(turn * (q1 * l0[None, :]) / WIDTH), (1, OWN))
    twist[1, :, : OWN * STRIP] = np.tile(np.sin(turn * (q1 * l0[None, :]) / WIDTH), (1, OWN))
    inner = np.zeros((2, 256, 2, 256))
    for e in range(2):
        for r in range(OWN):
            h = np.arange(BLOCKS)[:, None]
            angle = turn * ((2 * h + e) * l0[None, :] % 32) / 32
            c, s = np.cos(angle) / WIDTH, np.sin(angle) / WIDTH
            re = slice(r * 32, r * 32 + 16)
            im = slice(r * 32 + 16, r * 32 + 32)
            cols = slice(r * STRIP, (r + 1) * STRIP)
            inner[e, re, 0, cols] = c
            inner[e, re, 1, cols] = s
            inner[e, im, 1, cols] = c
            inner[e, im, 0, cols] = -s
    inner = inner.reshape(512, 512)
    f32 = lambda x: np.asarray(x, np.float32)
    bf16 = lambda x: jnp.asarray(f32(x)).astype(BF16)
    return f32(coarse), f32(fine), bf16(outer), bf16(outer.T), f32(twist), bf16(inner)


def kernel(
    image_ref,
    pay_ref,
    table_ref,
    coarse_ref,
    fine_hbm,
    outer_ref,
    outer_t_ref,
    twist_ref,
    inner_ref,
    back_ref,
    grad_ref,
    fine,
    basis,
    half_out,
    half_in,
    pay_in,
    fields,
    grid_all,
    windows,
    taps_v,
    taps_u,
    deposit,
    model,
    back_out,
    part_out,
    part_in,
    col_out,
    col_in,
    dirty_out,
    dirty_in,
    fine_sem,
    send_sem,
    recv_sem,
):
    u = lax.axis_index("uv")
    f = lax.axis_index("freq")

    fine_copy = pltpu.make_async_copy(fine_hbm.at[f], fine, fine_sem)
    fine_copy.start()
    barrier = pltpu.get_barrier_semaphore()

    def greet_uv(k, carry):
        peer = lax.rem(u + k, TILES)
        pl.semaphore_signal(barrier, inc=1, device_id=(peer, f), device_id_type=MESH)
        return carry

    def greet_freq(k, carry):
        peer = lax.rem(f + k, GROUPS)
        pl.semaphore_signal(barrier, inc=1, device_id=(u, peer), device_id_type=MESH)
        return carry

    lax.fori_loop(1, TILES, greet_uv, 0)
    lax.fori_loop(1, GROUPS, greet_freq, 0)

    def scatter_uv(src, dst, which):
        def step(k, carry):
            peer = lax.rem(u + k, TILES)
            pltpu.make_async_remote_copy(
                src_ref=src.at[peer],
                dst_ref=dst.at[u],
                send_sem=send_sem.at[which],
                recv_sem=recv_sem.at[which],
                device_id=(peer, f),
                device_id_type=MESH,
            ).start()
            return carry

        lax.fori_loop(1, TILES, step, 0)

    def scatter_freq(src_at, dst, which):
        def step(k, carry):
            peer = lax.rem(f + k, GROUPS)
            pltpu.make_async_remote_copy(
                src_ref=src_at(peer),
                dst_ref=dst.at[f],
                send_sem=send_sem.at[which],
                recv_sem=recv_sem.at[which],
                device_id=(u, peer),
                device_id_type=MESH,
            ).start()
            return carry

        lax.fori_loop(1, GROUPS, step, 0)

    def all_but_one(dst, which, count):
        blocks = dst.at[pl.ds(0, count - 1)]
        return pltpu.make_async_remote_copy(
            src_ref=blocks,
            dst_ref=blocks,
            send_sem=send_sem.at[which],
            recv_sem=recv_sem.at[which],
            device_id=(u, f),
            device_id_type=MESH,
        )

    fine_copy.wait()
    cos_a, sin_a = coarse_ref[0], coarse_ref[1]

    def make_basis(t, carry):
        lanes = pl.ds(pl.multiple_of(t * 128, 128), 128)
        for r in range(OWN):
            cos_b, sin_b = fine[r : r + 1, lanes], fine[8 + r : 9 + r, lanes]
            basis[r * 128 : r * 128 + 64, lanes] = (cos_a * cos_b - sin_a * sin_b).astype(BF16)
            basis[r * 128 + 64 : r * 128 + 128, lanes] = (
                -(sin_a * cos_b) - cos_a * sin_b
            ).astype(BF16)
        return carry

    lax.fori_loop(0, WIDTH // 128, make_basis, 0)

    half = lax.dot_general(
        basis[...], image_ref[...], (((1,), (1,)), ((), ())), preferred_element_type=F32
    )
    blank = jnp.zeros((2 * TILES, 256 - OWN * STRIP), F32)
    half = jnp.concatenate([half[r * 128 : (r + 1) * 128] for r in range(OWN)] + [blank], axis=1)
    half_out[...] = jnp.stack([half[:TILES], half[TILES:]], axis=1).astype(BF16)

    pl.semaphore_wait(barrier, TILES + GROUPS - 2)
    scatter_uv(half_out, half_in, 0)
    scatter_uv(pay_ref, pay_in, 1)
    half_in[pl.ds(u, 1)] = half_out[pl.ds(u, 1)]
    pay_in[pl.ds(u, 1)] = pay_ref[pl.ds(u, 1)]
    windows_zero = jnp.zeros((112, TILES * SLOTS), BF16)
    taps_v[144:256] = windows_zero

    all_but_one(half_in, 0, TILES).wait()
    half = half_in[...].astype(F32)
    half = jnp.concatenate([half[:, 0], half[:, 1]], axis=0).astype(BF16)
    mixed = jnp.dot(outer_ref[...], half, preferred_element_type=F32)
    real, imag = mixed[:64], mixed[64:]
    cos_t, sin_t = twist_ref[0], twist_ref[1]
    mixed = jnp.concatenate(
        [real * cos_t + imag * sin_t, imag * cos_t - real * sin_t], axis=1
    ).astype(BF16)
    own = lax.dot_general(
        inner_ref[...], mixed, (((1,), (1,)), ((), ())), preferred_element_type=F32
    )
    own = jnp.concatenate([own[:PIECE], own[256 : 256 + PIECE]], axis=1).astype(BF16)
    grid_all[pl.ds(f, 1)] = own[None]
    scatter_freq(lambda peer: grid_all.at[f], grid_all, 2)

    all_but_one(pay_in, 1, TILES).wait()
    arrived = pay_in[...].astype(F32)
    arrived = jnp.concatenate([arrived[:, 0], arrived[:, 1]], axis=1).T
    for k in range(8):
        fields[k] = jnp.concatenate(
            [arrived[k * 32 + 8 * g : k * 32 + 8 * g + 8] for g in range(4)], axis=1
        )
    table = table_ref[...]
    table_high = table.astype(BF16)
    table_low = (table - table_high.astype(F32)).astype(BF16)
    table_both = jnp.concatenate([table_high.astype(F32), table_low.astype(F32)], axis=0).astype(BF16)
    table_narrow = jnp.concatenate([table_high.astype(F32), jnp.zeros((8, 128), F32)], axis=0).astype(BF16)

    def prepare(i, carry):
        lanes = pl.ds(pl.multiple_of(i * BATCH, BATCH), BATCH)
        row, offset_u = fields[2, pl.ds(i, 1), :], fields[3, pl.ds(i, 1), :]
        low, offset_v = fields[5, pl.ds(i, 1), :], fields[6, pl.ds(i, 1), :]
        position = lax.broadcasted_iota(jnp.int32, (128, BATCH), 0).astype(F32)
        hot_u = jnp.where(position == offset_u, 1.0, 0.0).astype(BF16)
        hot_v = jnp.where(position == offset_v, 1.0, 0.0).astype(BF16)
        both = jnp.dot(table_both, hot_u, preferred_element_type=F32)
        factor_u = both[:8] + both[8:]
        factor_v = jnp.dot(table_narrow, hot_v, preferred_element_type=F32)
        away = lax.broadcasted_iota(jnp.int32, (144, BATCH), 0).astype(F32) - low
        across = jnp.zeros((144, BATCH), F32)
        for t in range(TAPS):
            across = jnp.where(away == t, factor_v[t : t + 1], across)
        taps_v[0:144, lanes] = across.astype(BF16)
        away = lax.broadcasted_iota(jnp.int32, (40, BATCH), 0).astype(F32) - row
        down = jnp.zeros((40, BATCH), F32)
        for t in range(TAPS):
            down = jnp.where(away == t, factor_u[t : t + 1], down)
        taps_u[i] = down
        return carry

    lax.fori_loop(0, TILES * SLOTS // BATCH, prepare, 0)

    all_but_one(grid_all, 2, GROUPS).wait()
    for g in range(GROUPS):
        piece = grid_all[g]
        windows[g * PIECE : (g + 1) * PIECE, 0:128] = piece
        piece = piece.astype(F32).reshape(OWN * 2, BLOCKS, 128)
        piece = jnp.concatenate([piece[:, 1:], piece[:, :1]], axis=1)
        windows[g * PIECE : (g + 1) * PIECE, 128:256] = piece.reshape(PIECE, 128).astype(BF16)

    def visit(i, carry):
        lanes = pl.ds(pl.multiple_of(i * BATCH, BATCH), BATCH)
        sampled = jnp.dot(windows[...], taps_v[:, lanes], preferred_element_type=F32)
        total = jnp.zeros((2 * BLOCKS, BATCH), F32)
        for r in range(GROUPS * OWN):
            total = total + sampled[r * 32 : (r + 1) * 32] * taps_u[i, r : r + 1, :]
        block = fields[4, pl.ds(i, 1), :]
        here = lax.broadcasted_iota(jnp.int32, (BLOCKS, BATCH), 0).astype(F32) == block
        parts = []
        for c in range(2):
            found = jnp.where(here, total[c * BLOCKS : (c + 1) * BLOCKS], 0.0)
            found = jnp.sum(found, axis=0, keepdims=True)
            model[c, pl.ds(i, 1), :] = found
            parts.append(jnp.where(here, fields[c, pl.ds(i, 1), :] - found, 0.0))
        left = jnp.concatenate(parts, axis=0)
        for r in range(GROUPS * OWN):
            deposit[r * 32 : (r + 1) * 32, lanes] = (left * taps_u[i, r : r + 1, :]).astype(BF16)
        return carry

    lax.fori_loop(0, TILES * SLOTS // BATCH, visit, 0)

    rows = []
    for c in range(2):
        values = model[c]
        for g in range(4):
            rows.append(values[:, 64 * g : 64 * g + 64])
    rows.append(jnp.zeros((64, 64), F32))
    back_out[...] = jnp.concatenate(rows, axis=0).T.reshape(TILES, 1, 128)
    scatter_uv(back_out, back_ref, 3)
    back_ref[pl.ds(u, 1)] = back_out[pl.ds(u, 1)]

    spread = lax.dot_general(
        deposit[...], taps_v[...], (((1,), (1,)), ((), ())), preferred_element_type=F32
    )
    for g in range(GROUPS):
        piece = spread[g * PIECE : (g + 1) * PIECE]
        over = piece[:, 128:256].reshape(OWN * 2, BLOCKS, 128)
        over = jnp.concatenate([over[:, BLOCKS - 1 :], over[:, : BLOCKS - 1]], axis=1)
        part_out[g] = (piece[:, 0:128] + over.reshape(PIECE, 128)).astype(BF16)
    scatter_freq(lambda peer: part_out.at[peer], part_in, 4)
    part_in[pl.ds(f, 1)] = part_out[pl.ds(f, 1)]
    all_but_one(part_in, 4, GROUPS).wait()
    whole = part_in[0].astype(F32)
    for g in range(1, GROUPS):
        whole = whole + part_in[g].astype(F32)

    whole = jnp.concatenate([whole, jnp.zeros((256 - PIECE, 128), F32)], axis=0).T
    whole = jnp.concatenate([whole[:64], whole[64:]], axis=1).astype(BF16)
    mixed = jnp.dot(whole, inner_ref[...], preferred_element_type=F32)
    real, imag = mixed[:, :256], mixed[:, 256:]
    mixed = jnp.concatenate(
        [real * cos_t - imag * sin_t, imag * cos_t + real * sin_t], axis=0
    ).astype(BF16)
    column = jnp.dot(outer_t_ref[...], mixed, preferred_element_type=F32)
    col_out[...] = jnp.stack([column[:TILES], column[TILES:]], axis=1).astype(BF16)
    scatter_uv(col_out, col_in, 5)
    col_in[pl.ds(u, 1)] = col_out[pl.ds(u, 1)]
    all_but_one(col_in, 5, TILES).wait()

    column = col_in[...].astype(F32)
    column = jnp.concatenate([column[:, 0], column[:, 1]], axis=0).T
    column = jnp.concatenate(
        [column[r * STRIP : (r + 1) * STRIP] for r in range(OWN)], axis=1
    ).astype(BF16)
    dirty = jnp.dot(column, basis[...], preferred_element_type=F32)
    for g in range(GROUPS):
        dirty_out[g] = dirty[:, g * 256 : (g + 1) * 256].astype(BF16)
    scatter_freq(lambda peer: dirty_out.at[peer], dirty_in, 6)
    dirty_in[pl.ds(f, 1)] = dirty_out[pl.ds(f, 1)]
    all_but_one(dirty_in, 6, GROUPS).wait()
    image = dirty_in[0].astype(F32)
    for g in range(1, GROUPS):
        image = image + dirty_in[g].astype(F32)
    grad_ref[...] = image
    all_but_one(back_ref, 3, TILES).wait()


def per_device(
    model_image, visibilities, cell_rows, cell_cols, kernel_offsets, slot_counts, kernel_table
):
    values = visibilities.reshape(2, TILES, SLOTS)
    cols = cell_cols.reshape(TILES, SLOTS)
    offsets = kernel_offsets.reshape(2, TILES, SLOTS)
    live = jnp.arange(SLOTS, dtype=jnp.int32)[None, :] < slot_counts.reshape(TILES, 1)
    first = [
        values[0],
        values[1],
        cell_rows.reshape(TILES, SLOTS).astype(F32),
        jnp.where(live, offsets[0], -1).astype(F32),
    ]
    second = [
        (cols // 128).astype(F32),
        (cols % 128).astype(F32),
        offsets[1].astype(F32),
        jnp.zeros((TILES, SLOTS), F32),
    ]
    payload = jnp.stack(
        [jnp.concatenate(first, axis=1), jnp.concatenate(second, axis=1)], axis=1
    ).astype(BF16)

    coarse, fine, outer, outer_t, twist, inner = tables()
    vmem = pl.BlockSpec(memory_space=pltpu.VMEM)
    count = TILES * SLOTS // BATCH
    back, gradient = pl.pallas_call(
        kernel,
        out_shape=(
            jax.ShapeDtypeStruct((TILES, 1, 128), F32),
            jax.ShapeDtypeStruct((STRIP, WIDTH // GROUPS), F32),
        ),
        in_specs=[vmem] * 4 + [pl.BlockSpec(memory_space=pl.ANY)] + [vmem] * 4,
        out_specs=(vmem, vmem),
        scratch_shapes=[
            pltpu.VMEM((16, WIDTH), F32),
            pltpu.VMEM((OWN * 128, WIDTH), BF16),
            pltpu.VMEM((TILES, 2, 256), BF16),
            pltpu.VMEM((TILES, 2, 256), BF16),
            pltpu.VMEM((TILES, 2, 128), BF16),
            pltpu.VMEM((8, count, BATCH), F32),
            pltpu.VMEM((GROUPS, PIECE, 128), BF16),
            pltpu.VMEM((ROWS, 256), BF16),
            pltpu.VMEM((256, TILES * SLOTS), BF16),
            pltpu.VMEM((count, GROUPS * OWN, BATCH), F32),
            pltpu.VMEM((ROWS, TILES * SLOTS), BF16),
            pltpu.VMEM((2, count, BATCH), F32),
            pltpu.VMEM((TILES, 1, 128), F32),
            pltpu.VMEM((GROUPS, PIECE, 128), BF16),
            pltpu.VMEM((GROUPS, PIECE, 128), BF16),
            pltpu.VMEM((TILES, 2, 256), BF16),
            pltpu.VMEM((TILES, 2, 256), BF16),
            pltpu.VMEM((GROUPS, STRIP, WIDTH // GROUPS), BF16),
            pltpu.VMEM((GROUPS, STRIP, WIDTH // GROUPS), BF16),
            pltpu.SemaphoreType.DMA,
            pltpu.SemaphoreType.DMA((7,)),
            pltpu.SemaphoreType.DMA((7,)),
        ],
        compiler_params=pltpu.CompilerParams(
            collective_id=0, has_side_effects=True, vmem_limit_bytes=48 << 20
        ),
    )(
        model_image,
        payload,
        kernel_table.T,
        jnp.asarray(coarse),
        jnp.asarray(fine),
        outer,
        outer_t,
        jnp.asarray(twist),
        inner,
    )
    sampled = back.reshape(TILES, 128)[:, : 2 * SLOTS].reshape(TILES, 2, SLOTS).transpose(1, 0, 2)
    residual = jnp.where(live[None], values - sampled, 0.0)
    return residual.reshape(2, 1, 1, TILES, SLOTS), gradient


def solution(mesh):
    placed = (
        P("uv", None),
        P(None, "uv", "freq", None, None),
        P("uv", "freq", None, None),
        P("uv", "freq", None, None),
        P(None, "uv", "freq", None, None),
        P("uv", "freq", None),
        P(),
    )
    return jax.shard_map(
        per_device,
        mesh=mesh,
        in_specs=placed,
        out_specs=(P(None, "uv", "freq", None, None), P("uv", "freq")),
        check_vma=False,
    )
```

```python
import functools

import jax
import jax.numpy as jnp
import numpy as np
from jax import lax
from jax.experimental import pallas as pl
from jax.experimental.pallas import tpu as pltpu
from jax.sharding import PartitionSpec as P

MESH = pl.DeviceIdType.MESH
WIDTH = 2048
TILES = 64
GROUPS = 8
STRIP = 32
OWN = 5
SLOTS = 32
TAPS = 8
BLOCKS = 16
ROWS = GROUPS * OWN * 2 * BLOCKS
PIECE = OWN * 2 * BLOCKS
BATCH = 256
F32 = jnp.float32
BF16 = jnp.bfloat16


def tables():
    turn = 2.0 * np.pi
    v = np.arange(TILES)[:, None]
    m = np.arange(128)[None, :]
    coarse = np.stack([np.cos(turn * (v * m % 64) / 64), np.sin(turn * (v * m % 64) / 64)])
    rows = np.arange(GROUPS * OWN)[:, None] * np.arange(WIDTH)[None, :] % WIDTH
    fine = np.zeros((GROUPS, 16, WIDTH))
    fine[:, 0:OWN] = np.cos(turn * rows / WIDTH).reshape(GROUPS, OWN, WIDTH)
    fine[:, 8 : 8 + OWN] = np.sin(turn * rows / WIDTH).reshape(GROUPS, OWN, WIDTH)
    q1 = np.arange(64)[:, None]
    u = np.arange(64)[None, :]
    cos64, sin64 = np.cos(turn * (q1 * u % 64) / 64), np.sin(turn * (q1 * u % 64) / 64)
    outer = np.block([[cos64, sin64], [-sin64, cos64]])
    l0 = np.arange(STRIP)
    twist = np.zeros((2, 64, 256))
    twist[0, :, : OWN * STRIP] = np.tile(np.cos(turn * (q1 * l0[None, :]) / WIDTH), (1, OWN))
    twist[1, :, : OWN * STRIP] = np.tile(np.sin(turn * (q1 * l0[None, :]) / WIDTH), (1, OWN))
    inner = np.zeros((2, 256, 2, 256))
    for e in range(2):
        for r in range(OWN):
            h = np.arange(BLOCKS)[:, None]
            angle = turn * ((2 * h + e) * l0[None, :] % 32) / 32
            c, s = np.cos(angle) / WIDTH, np.sin(angle) / WIDTH
            re = slice(r * 32, r * 32 + 16)
            im = slice(r * 32 + 16, r * 32 + 32)
            cols = slice(r * STRIP, (r + 1) * STRIP)
            inner[e, re, 0, cols] = c
            inner[e, re, 1, cols] = s
            inner[e, im, 1, cols] = c
            inner[e, im, 0, cols] = -s
    inner = inner.reshape(512, 512)
    f32 = lambda x: np.asarray(x, np.float32)
    bf16 = lambda x: jnp.asarray(f32(x)).astype(BF16)
    return f32(coarse), f32(fine), bf16(outer), bf16(outer.T), f32(twist), bf16(inner)


def kernel(
    image_hbm,
    vis_hbm,
    rows_hbm,
    cols_hbm,
    offsets_hbm,
    counts_hbm,
    table_hbm,
    coarse_hbm,
    fine_hbm,
    outer_hbm,
    outer_t_hbm,
    twist_hbm,
    inner_hbm,
    residual_ref,
    grad_ref,
    image,
    vis,
    cell_rows,
    cell_cols,
    offsets,
    counts,
    table_in,
    coarse,
    fine,
    outer,
    outer_t,
    twist,
    inner,
    basis,
    half_out,
    half_in,
    pay_out,
    pay_in,
    fields,
    grid_all,
    windows,
    taps_v,
    taps_t,
    taps_u,
    totals,
    deposit,
    model,
    back_out,
    back_in,
    part_out,
    part_in,
    col_out,
    col_in,
    dirty_out,
    dirty_in,
    load_sem,
    send_sem,
    recv_sem,
    near_send,
    near_recv,
):
    u = lax.axis_index("uv")
    f = lax.axis_index("freq")
    chip, core = f // 2, lax.rem(f, 2)
    batches = TILES * SLOTS // BATCH

    loads = []
    for n, (source, target) in enumerate(
        [
            (image_hbm, image),
            (coarse_hbm, coarse),
            (fine_hbm.at[f], fine),
            (vis_hbm, vis),
            (rows_hbm, cell_rows),
            (cols_hbm, cell_cols),
            (offsets_hbm, offsets),
            (counts_hbm, counts),
            (table_hbm, table_in),
            (outer_hbm, outer),
            (twist_hbm, twist),
            (inner_hbm, inner),
            (outer_t_hbm, outer_t),
        ]
    ):
        load = pltpu.make_async_copy(source, target, load_sem.at[n])
        load.start()
        loads.append(load)
    barrier = pltpu.get_barrier_semaphore()

    def peer_uv(j):
        away = (j + 1) // 2
        return lax.rem(u + TILES // 2 + away * (2 * lax.rem(j, 2) - 1) + TILES, TILES)

    def greet_uv(j, carry):
        pl.semaphore_signal(barrier, inc=1, device_id=(peer_uv(j), f), device_id_type=MESH)
        return carry

    lax.fori_loop(0, TILES - 1, greet_uv, 0)

    def at(dx, dc):
        return 2 * lax.rem(chip + dx, 4) + lax.rem(core + dc, 2)

    for dx in (2, 1, 3, 0):
        for dc in (0, 1):
            if dx or dc:
                pl.semaphore_signal(
                    barrier, inc=1, device_id=(u, at(dx, dc)), device_id_type=MESH
                )

    def scatter_uv(src, dst, which):
        def step(j, carry):
            peer = peer_uv(j)
            pltpu.make_async_remote_copy(
                src_ref=src.at[peer],
                dst_ref=dst.at[u],
                send_sem=send_sem.at[which],
                recv_sem=recv_sem.at[which],
                device_id=(peer, f),
                device_id_type=MESH,
            ).start()
            return carry

        lax.fori_loop(0, TILES - 1, step, 0)

    def all_but_one(dst, which):
        blocks = dst.at[pl.ds(0, TILES - 1)]
        return pltpu.make_async_remote_copy(
            src_ref=blocks,
            dst_ref=blocks,
            send_sem=send_sem.at[which],
            recv_sem=recv_sem.at[which],
            device_id=(u, f),
            device_id_type=MESH,
        )

    def send_near(src, dst, which, dx, dc):
        copy = pltpu.make_async_remote_copy(
            src_ref=src,
            dst_ref=dst.at[f],
            send_sem=near_send.at[which, 2 * dx + dc],
            recv_sem=near_recv.at[which, 2 * dx + dc],
            device_id=(u, at(dx, dc)),
            device_id_type=MESH,
        )
        copy.start()
        return copy

    for n in range(3):
        loads[n].wait()
    cos_a, sin_a = coarse[0], coarse[1]

    def make_basis(t, carry):
        lanes = pl.ds(pl.multiple_of(t * 128, 128), 128)
        for r in range(OWN):
            cos_b, sin_b = fine[r : r + 1, lanes], fine[8 + r : 9 + r, lanes]
            basis[r * 128 : r * 128 + 64, lanes] = (cos_a * cos_b - sin_a * sin_b).astype(BF16)
            basis[r * 128 + 64 : r * 128 + 128, lanes] = (
                -(sin_a * cos_b) - cos_a * sin_b
            ).astype(BF16)
        return carry

    lax.fori_loop(0, WIDTH // 128, make_basis, 0)
    half = lax.dot_general(
        basis[...], image[...], (((1,), (1,)), ((), ())), preferred_element_type=F32
    )
    blank = jnp.zeros((2 * TILES, 256 - OWN * STRIP), F32)
    half = jnp.concatenate([half[r * 128 : (r + 1) * 128] for r in range(OWN)] + [blank], axis=1)
    half_out[...] = jnp.stack([half[:TILES], half[TILES:]], axis=1).astype(BF16)

    for n in range(3, len(loads)):
        loads[n].wait()
    slot = lax.broadcasted_iota(jnp.int32, (SLOTS, TILES), 0)
    live = slot < counts[...]
    cols = cell_cols[...]
    high = lax.shift_right_logical(cols, 7)
    packed = jnp.concatenate(
        [
            vis[0],
            vis[1],
            cell_rows[...].astype(F32),
            jnp.where(live, offsets[0], -1).astype(F32),
            high.astype(F32),
            (cols - high * 128).astype(F32),
            offsets[1].astype(F32),
            jnp.zeros((SLOTS, TILES), F32),
        ],
        axis=0,
    ).T
    pay_out[...] = jnp.stack([packed[:, :128], packed[:, 128:]], axis=1).astype(BF16)

    pl.semaphore_wait(barrier, TILES + GROUPS - 2)
    scatter_uv(half_out, half_in, 0)
    scatter_uv(pay_out, pay_in, 1)
    half_in[pl.ds(u, 1)] = half_out[pl.ds(u, 1)]
    pay_in[pl.ds(u, 1)] = pay_out[pl.ds(u, 1)]
    taps_v[144:256] = jnp.zeros((112, TILES * SLOTS), BF16)
    totals[...] = jnp.zeros_like(totals)

    all_but_one(half_in, 0).wait()
    half = half_in[...].astype(F32)
    half = jnp.concatenate([half[:, 0], half[:, 1]], axis=0).astype(BF16)
    mixed = jnp.dot(outer[...], half, preferred_element_type=F32)
    real, imag = mixed[:64], mixed[64:]
    cos_t, sin_t = twist[0], twist[1]
    mixed = jnp.concatenate(
        [real * cos_t + imag * sin_t, imag * cos_t - real * sin_t], axis=1
    ).astype(BF16)
    own = lax.dot_general(
        inner[...], mixed, (((1,), (1,)), ((), ())), preferred_element_type=F32
    )
    own = jnp.concatenate([own[:PIECE], own[256 : 256 + PIECE]], axis=1).astype(BF16)
    grid_all[pl.ds(f, 1)] = own[None]
    pieces = {}
    for dx in (2, 1, 3, 0):
        for dc in (0, 1):
            if dx or dc:
                pieces[dx, dc] = send_near(grid_all.at[f], grid_all, 0, dx, dc)

    all_but_one(pay_in, 1).wait()
    arrived = pay_in[...].astype(F32)
    arrived = jnp.concatenate([arrived[:, 0], arrived[:, 1]], axis=1).T
    for k in range(8):
        fields[k] = jnp.concatenate(
            [arrived[k * 32 + 8 * g : k * 32 + 8 * g + 8] for g in range(4)], axis=1
        )
    table = table_in[...]
    table_high = table.astype(BF16)
    table_low = (table - table_high.astype(F32)).astype(BF16)
    table_both = jnp.concatenate([table_high.astype(F32), table_low.astype(F32)], axis=0).astype(BF16)
    table_narrow = jnp.concatenate([table_high.astype(F32), jnp.zeros((8, 128), F32)], axis=0).astype(BF16)

    def prepare(i, carry):
        lanes = pl.ds(pl.multiple_of(i * BATCH, BATCH), BATCH)
        row, offset_u = fields[2, pl.ds(i, 1), :], fields[3, pl.ds(i, 1), :]
        low, offset_v = fields[5, pl.ds(i, 1), :], fields[6, pl.ds(i, 1), :]
        position = lax.broadcasted_iota(jnp.int32, (128, BATCH), 0).astype(F32)
        hot_u = jnp.where(position == offset_u, 1.0, 0.0).astype(BF16)
        hot_v = jnp.where(position == offset_v, 1.0, 0.0).astype(BF16)
        both = jnp.dot(table_both, hot_u, preferred_element_type=F32)
        factor_u = both[:8] + both[8:]
        factor_v = jnp.dot(table_narrow, hot_v, preferred_element_type=F32)
        away = lax.broadcasted_iota(jnp.int32, (144, BATCH), 0).astype(F32) - low
        across = jnp.zeros((144, BATCH), F32)
        for t in range(TAPS):
            across = jnp.where(away == t, factor_v[t : t + 1], across)
        taps_v[0:144, lanes] = across.astype(BF16)
        across = jnp.concatenate([across, jnp.zeros((112, BATCH), F32)], axis=0)
        taps_t[lanes, :] = across.T.astype(BF16)
        place = lax.broadcasted_iota(jnp.int32, (64, BATCH), 0)
        group = lax.shift_right_logical(place, 3)
        away = (group * OWN + place - group * 8).astype(F32) - row
        down = jnp.zeros((64, BATCH), F32)
        for t in range(TAPS):
            down = jnp.where(away == t, factor_u[t : t + 1], down)
        taps_u[i] = down.reshape(GROUPS, 8, BATCH)
        return carry

    lax.fori_loop(0, batches, prepare, 0)

    for dx in (0, 1, 3, 2):
        there = lax.rem(chip - dx + 4, 4)
        for dc in (0, 1):
            if dx or dc:
                pieces[dx, dc].wait_recv()
        for side in range(2):
            lines = pl.ds(side * PIECE, PIECE)
            piece = grid_all[pl.ds(2 * there + side, 1)].reshape(PIECE, 128)
            windows[there, lines, 0:128] = piece
            piece = piece.astype(F32).reshape(OWN * 2, BLOCKS, 128)
            piece = jnp.concatenate([piece[:, 1:], piece[:, :1]], axis=1)
            windows[there, lines, 128:256] = piece.reshape(PIECE, 128).astype(BF16)

        def sample(i, carry):
            lanes = pl.ds(pl.multiple_of(i * BATCH, BATCH), BATCH)
            sampled = jnp.dot(windows[there], taps_v[:, lanes], preferred_element_type=F32)
            total = totals[i]
            for side in range(2):
                taps = taps_u[i, pl.ds(2 * there + side, 1)].reshape(8, BATCH)
                for r in range(OWN):
                    n = (side * OWN + r) * 32
                    total = total + sampled[n : n + 32] * taps[r : r + 1]
            totals[i] = total
            return carry

        lax.fori_loop(0, batches, sample, 0)

    def visit(i, carry):
        lanes = pl.ds(pl.multiple_of(i * BATCH, BATCH), BATCH)
        block = fields[4, pl.ds(i, 1), :]
        here = lax.broadcasted_iota(jnp.int32, (BLOCKS, BATCH), 0).astype(F32) == block
        parts = []
        for c in range(2):
            found = jnp.where(here, totals[i, c * BLOCKS : (c + 1) * BLOCKS], 0.0)
            found = jnp.sum(found, axis=0, keepdims=True)
            model[c, pl.ds(i, 1), :] = found
            parts.append(jnp.where(here, fields[c, pl.ds(i, 1), :] - found, 0.0))
        left = jnp.concatenate(parts, axis=0)
        for g in range(GROUPS):
            taps = taps_u[i, g]
            for r in range(OWN):
                n = (g % 2 * OWN + r) * 32
                deposit[g // 2, n : n + 32, lanes] = (left * taps[r : r + 1]).astype(BF16)
        return carry

    lax.fori_loop(0, batches, visit, 0)

    sums = {}
    for dx in (2, 1, 3, 0):
        there = lax.rem(chip + dx, 4)
        spread = jnp.dot(deposit[there], taps_t[...], preferred_element_type=F32)
        for side in range(2):
            piece = spread[side * PIECE : (side + 1) * PIECE]
            over = piece[:, 128:256].reshape(OWN * 2, BLOCKS, 128)
            over = jnp.concatenate([over[:, BLOCKS - 1 :], over[:, : BLOCKS - 1]], axis=1)
            piece = (piece[:, 0:128] + over.reshape(PIECE, 128)).astype(BF16)
            part_out[pl.ds(2 * there + side, 1)] = piece[None]
        for dc in (0, 1):
            if dx or dc:
                sums[dx, dc] = send_near(part_out.at[at(dx, dc)], part_in, 1, dx, dc)
    part_in[pl.ds(f, 1)] = part_out[pl.ds(f, 1)]

    lines = []
    for c in range(2):
        values = model[c]
        for g in range(4):
            lines.append(values[:, 64 * g : 64 * g + 64])
    lines.append(jnp.zeros((64, 64), F32))
    back_out[...] = jnp.concatenate(lines, axis=0).T.reshape(TILES, 1, 128)
    scatter_uv(back_out, back_in, 2)
    back_in[pl.ds(u, 1)] = back_out[pl.ds(u, 1)]

    for copy in sums.values():
        copy.wait_recv()
    whole = part_in[0].astype(F32)
    for g in range(1, GROUPS):
        whole = whole + part_in[g].astype(F32)

    whole = jnp.concatenate([whole, jnp.zeros((256 - PIECE, 128), F32)], axis=0).T
    whole = jnp.concatenate([whole[:64], whole[64:]], axis=1).astype(BF16)
    mixed = jnp.dot(whole, inner[...], preferred_element_type=F32)
    real, imag = mixed[:, :256], mixed[:, 256:]
    mixed = jnp.concatenate(
        [real * cos_t - imag * sin_t, imag * cos_t + real * sin_t], axis=0
    ).astype(BF16)
    column = jnp.dot(outer_t[...], mixed, preferred_element_type=F32)
    col_out[...] = jnp.stack([column[:TILES], column[TILES:]], axis=1).astype(BF16)
    scatter_uv(col_out, col_in, 3)
    col_in[pl.ds(u, 1)] = col_out[pl.ds(u, 1)]

    all_but_one(back_in, 2).wait()
    sampled = back_in[...].reshape(TILES, 128).T
    for c in range(2):
        residual_ref[c] = jnp.where(
            slot < counts[...], vis[c] - sampled[c * SLOTS : (c + 1) * SLOTS], 0.0
        )
    for copies in (pieces, sums):
        for copy in copies.values():
            copy.wait_send()

    all_but_one(col_in, 3).wait()
    column = col_in[...].astype(F32)
    column = jnp.concatenate([column[:, 0], column[:, 1]], axis=0).T
    column = jnp.concatenate(
        [column[r * STRIP : (r + 1) * STRIP] for r in range(OWN)], axis=1
    ).astype(BF16)
    shares = {}
    for dx in (2, 1, 3, 0):
        there = lax.rem(chip + dx, 4)
        lanes = pl.ds(pl.multiple_of(there * 512, 512), 512)
        dirty = jnp.dot(column, basis[:, lanes], preferred_element_type=F32)
        for side in range(2):
            piece = dirty[:, side * 256 : (side + 1) * 256].astype(BF16)
            dirty_out[pl.ds(2 * there + side, 1)] = piece[None]
        for dc in (0, 1):
            if dx or dc:
                shares[dx, dc] = send_near(dirty_out.at[at(dx, dc)], dirty_in, 2, dx, dc)
    dirty_in[pl.ds(f, 1)] = dirty_out[pl.ds(f, 1)]
    for copy in shares.values():
        copy.wait()
    picture = dirty_in[0].astype(F32)
    for g in range(1, GROUPS):
        picture = picture + dirty_in[g].astype(F32)
    grad_ref[...] = picture


def per_device(
    model_image, visibilities, cell_rows, cell_cols, kernel_offsets, slot_counts, kernel_table
):
    constants = [jnp.asarray(x) for x in tables()]
    inputs = [
        model_image,
        visibilities.reshape(2, TILES, SLOTS).transpose(0, 2, 1),
        cell_rows.reshape(TILES, SLOTS).T,
        cell_cols.reshape(TILES, SLOTS).T,
        kernel_offsets.reshape(2, TILES, SLOTS).transpose(0, 2, 1),
        slot_counts.reshape(1, TILES),
        kernel_table.T,
    ] + constants
    vmem = pl.BlockSpec(memory_space=pltpu.VMEM)
    hbm = pl.BlockSpec(memory_space=pltpu.HBM)
    batches = TILES * SLOTS // BATCH
    local = [pltpu.VMEM(x.shape[1:] if n == 8 else x.shape, x.dtype) for n, x in enumerate(inputs)]
    residual, gradient = pl.pallas_call(
        kernel,
        out_shape=(
            jax.ShapeDtypeStruct((2, SLOTS, TILES), F32),
            jax.ShapeDtypeStruct((STRIP, WIDTH // GROUPS), F32),
        ),
        in_specs=[hbm] * len(inputs),
        out_specs=(vmem, vmem),
        scratch_shapes=local
        + [
            pltpu.VMEM((OWN * 128, WIDTH), BF16),
            pltpu.VMEM((TILES, 2, 256), BF16),
            pltpu.VMEM((TILES, 2, 256), BF16),
            pltpu.VMEM((TILES, 2, 128), BF16),
            pltpu.VMEM((TILES, 2, 128), BF16),
            pltpu.VMEM((8, batches, BATCH), F32),
            pltpu.VMEM((GROUPS, PIECE, 128), BF16),
            pltpu.VMEM((4, 2 * PIECE, 256), BF16),
            pltpu.VMEM((256, TILES * SLOTS), BF16),
            pltpu.VMEM((TILES * SLOTS, 256), BF16),
            pltpu.VMEM((batches, GROUPS, 8, BATCH), F32),
            pltpu.VMEM((batches, 2 * BLOCKS, BATCH), F32),
            pltpu.VMEM((4, 2 * PIECE, TILES * SLOTS), BF16),
            pltpu.VMEM((2, batches, BATCH), F32),
            pltpu.VMEM((TILES, 1, 128), F32),
            pltpu.VMEM((TILES, 1, 128), F32),
            pltpu.VMEM((GROUPS, PIECE, 128), BF16),
            pltpu.VMEM((GROUPS, PIECE, 128), BF16),
            pltpu.VMEM((TILES, 2, 256), BF16),
            pltpu.VMEM((TILES, 2, 256), BF16),
            pltpu.VMEM((GROUPS, STRIP, WIDTH // GROUPS), BF16),
            pltpu.VMEM((GROUPS, STRIP, WIDTH // GROUPS), BF16),
            pltpu.SemaphoreType.DMA((len(inputs),)),
            pltpu.SemaphoreType.DMA((4,)),
            pltpu.SemaphoreType.DMA((4,)),
            pltpu.SemaphoreType.DMA((3, GROUPS)),
            pltpu.SemaphoreType.DMA((3, GROUPS)),
        ],
        compiler_params=pltpu.CompilerParams(
            collective_id=0, has_side_effects=True, vmem_limit_bytes=60 << 20
        ),
    )(*inputs)
    return residual.transpose(0, 2, 1).reshape(2, 1, 1, TILES, SLOTS), gradient


def solution(mesh):
    placed = (
        P("uv", None),
        P(None, "uv", "freq", None, None),
        P("uv", "freq", None, None),
        P("uv", "freq", None, None),
        P(None, "uv", "freq", None, None),
        P("uv", "freq", None),
        P(),
    )
    return jax.shard_map(
        per_device,
        mesh=mesh,
        in_specs=placed,
        out_specs=(P(None, "uv", "freq", None, None), P("uv", "freq")),
        check_vma=False,
    )
```

```python
import functools

import jax
import jax.numpy as jnp
import numpy as np
from jax import lax
from jax.experimental import pallas as pl
from jax.experimental.pallas import tpu as pltpu
from jax.sharding import PartitionSpec as P

MESH = pl.DeviceIdType.MESH
WIDTH = 2048
TILES = 64
GROUPS = 8
STRIP = 32
OWN = 5
SLOTS = 32
TAPS = 8
BLOCKS = 16
ROWS = GROUPS * OWN * 2 * BLOCKS
PIECE = OWN * 2 * BLOCKS
BATCH = 256
F32 = jnp.float32
BF16 = jnp.bfloat16


def tables():
    turn = 2.0 * np.pi
    v = np.arange(TILES)[:, None]
    m = np.arange(128)[None, :]
    coarse = np.stack([np.cos(turn * (v * m % 64) / 64), np.sin(turn * (v * m % 64) / 64)])
    rows = np.arange(GROUPS * OWN)[:, None] * np.arange(WIDTH)[None, :] % WIDTH
    fine = np.zeros((GROUPS, 16, WIDTH))
    fine[:, 0:OWN] = np.cos(turn * rows / WIDTH).reshape(GROUPS, OWN, WIDTH)
    fine[:, 8 : 8 + OWN] = np.sin(turn * rows / WIDTH).reshape(GROUPS, OWN, WIDTH)
    q1 = np.arange(64)[:, None]
    u = np.arange(64)[None, :]
    cos64, sin64 = np.cos(turn * (q1 * u % 64) / 64), np.sin(turn * (q1 * u % 64) / 64)
    outer = np.block([[cos64, sin64], [-sin64, cos64]])
    l0 = np.arange(STRIP)
    twist = np.zeros((2, 64, 256))
    twist[0, :, : OWN * STRIP] = np.tile(np.cos(turn * (q1 * l0[None, :]) / WIDTH), (1, OWN))
    twist[1, :, : OWN * STRIP] = np.tile(np.sin(turn * (q1 * l0[None, :]) / WIDTH), (1, OWN))
    inner = np.zeros((2, 256, 2, 256))
    for e in range(2):
        for r in range(OWN):
            h = np.arange(BLOCKS)[:, None]
            angle = turn * ((2 * h + e) * l0[None, :] % 32) / 32
            c, s = np.cos(angle) / WIDTH, np.sin(angle) / WIDTH
            re = slice(r * 32, r * 32 + 16)
            im = slice(r * 32 + 16, r * 32 + 32)
            cols = slice(r * STRIP, (r + 1) * STRIP)
            inner[e, re, 0, cols] = c
            inner[e, re, 1, cols] = s
            inner[e, im, 1, cols] = c
            inner[e, im, 0, cols] = -s
    inner = inner.reshape(512, 512)
    f32 = lambda x: np.asarray(x, np.float32)
    bf16 = lambda x: jnp.asarray(f32(x)).astype(BF16)
    return f32(coarse), f32(fine), bf16(outer), bf16(outer.T), f32(twist), bf16(inner)


def kernel(
    image_hbm,
    vis_hbm,
    rows_hbm,
    cols_hbm,
    offsets_hbm,
    counts_hbm,
    table_hbm,
    coarse_hbm,
    fine_hbm,
    outer_hbm,
    outer_t_hbm,
    twist_hbm,
    inner_hbm,
    residual_ref,
    grad_ref,
    image,
    vis,
    cell_rows,
    cell_cols,
    offsets,
    counts,
    table_in,
    coarse,
    fine,
    outer,
    outer_t,
    twist,
    inner,
    basis,
    half_out,
    half_in,
    pay_out,
    pay_in,
    fields,
    grid_all,
    windows,
    taps_v,
    taps_t,
    taps_u,
    totals,
    deposit,
    model,
    back_out,
    back_in,
    part_out,
    part_in,
    col_out,
    col_in,
    dirty_out,
    dirty_in,
    load_sem,
    send_sem,
    recv_sem,
    near_send,
    near_recv,
):
    u = lax.axis_index("uv")
    f = lax.axis_index("freq")
    chip, core = f // 2, lax.rem(f, 2)
    batches = TILES * SLOTS // BATCH

    loads = []
    for n, (source, target) in enumerate(
        [
            (image_hbm, image),
            (coarse_hbm, coarse),
            (fine_hbm.at[f], fine),
            (vis_hbm, vis),
            (rows_hbm, cell_rows),
            (cols_hbm, cell_cols),
            (offsets_hbm, offsets),
            (counts_hbm, counts),
            (table_hbm, table_in),
            (outer_hbm, outer),
            (twist_hbm, twist),
            (inner_hbm, inner),
            (outer_t_hbm, outer_t),
        ]
    ):
        load = pltpu.make_async_copy(source, target, load_sem.at[n])
        load.start()
        loads.append(load)
    barrier = pltpu.get_barrier_semaphore()

    def peer_uv(j):
        away = (j + 1) // 2
        return lax.rem(u + TILES // 2 + away * (2 * lax.rem(j, 2) - 1) + TILES, TILES)

    def greet_uv(j, carry):
        pl.semaphore_signal(barrier, inc=1, device_id=(peer_uv(j), f), device_id_type=MESH)
        return carry

    lax.fori_loop(0, TILES - 1, greet_uv, 0)

    def at(dx, dc):
        return 2 * lax.rem(chip + dx, 4) + lax.rem(core + dc, 2)

    for dx in (2, 1, 3, 0):
        for dc in (0, 1):
            if dx or dc:
                pl.semaphore_signal(
                    barrier, inc=1, device_id=(u, at(dx, dc)), device_id_type=MESH
                )

    def scatter_uv(src, dst, which):
        def step(j, carry):
            peer = peer_uv(j)
            pltpu.make_async_remote_copy(
                src_ref=src.at[peer],
                dst_ref=dst.at[u],
                send_sem=send_sem.at[which],
                recv_sem=recv_sem.at[which],
                device_id=(peer, f),
                device_id_type=MESH,
            ).start()
            return carry

        lax.fori_loop(0, TILES - 1, step, 0)

    def all_but_one(dst, which):
        blocks = dst.at[pl.ds(0, TILES - 1)]
        return pltpu.make_async_remote_copy(
            src_ref=blocks,
            dst_ref=blocks,
            send_sem=send_sem.at[which],
            recv_sem=recv_sem.at[which],
            device_id=(u, f),
            device_id_type=MESH,
        )

    def send_near(src, dst, which, dx, dc):
        copy = pltpu.make_async_remote_copy(
            src_ref=src,
            dst_ref=dst.at[f],
            send_sem=near_send.at[which, 2 * dx + dc],
            recv_sem=near_recv.at[which, 2 * dx + dc],
            device_id=(u, at(dx, dc)),
            device_id_type=MESH,
        )
        copy.start()
        return copy

    for n in range(3):
        loads[n].wait()
    cos_a, sin_a = coarse[0], coarse[1]

    def make_basis(t, carry):
        lanes = pl.ds(pl.multiple_of(t * 128, 128), 128)
        for r in range(OWN):
            cos_b, sin_b = fine[r : r + 1, lanes], fine[8 + r : 9 + r, lanes]
            basis[r * 128 : r * 128 + 64, lanes] = (cos_a * cos_b - sin_a * sin_b).astype(BF16)
            basis[r * 128 + 64 : r * 128 + 128, lanes] = (
                -(sin_a * cos_b) - cos_a * sin_b
            ).astype(BF16)
        return carry

    lax.fori_loop(0, WIDTH // 128, make_basis, 0, unroll=2)
    half = lax.dot_general(
        basis[...], image[...], (((1,), (1,)), ((), ())), preferred_element_type=F32
    )
    blank = jnp.zeros((2 * TILES, 256 - OWN * STRIP), F32)
    half = jnp.concatenate([half[r * 128 : (r + 1) * 128] for r in range(OWN)] + [blank], axis=1)
    half_out[...] = jnp.stack([half[:TILES], half[TILES:]], axis=1).astype(BF16)

    for n in range(3, len(loads)):
        loads[n].wait()
    slot = lax.broadcasted_iota(jnp.int32, (SLOTS, TILES), 0)
    live = slot < counts[...]
    cols = cell_cols[...]
    high = lax.shift_right_logical(cols, 7)
    packed = jnp.concatenate(
        [
            vis[0],
            vis[1],
            cell_rows[...].astype(F32),
            jnp.where(live, offsets[0], -1).astype(F32),
            high.astype(F32),
            (cols - high * 128).astype(F32),
            offsets[1].astype(F32),
            jnp.zeros((SLOTS, TILES), F32),
        ],
        axis=0,
    ).T
    pay_out[...] = jnp.stack([packed[:, :128], packed[:, 128:]], axis=1).astype(BF16)

    pl.semaphore_wait(barrier, TILES + GROUPS - 2)
    scatter_uv(half_out, half_in, 0)
    scatter_uv(pay_out, pay_in, 1)
    half_in[pl.ds(u, 1)] = half_out[pl.ds(u, 1)]
    pay_in[pl.ds(u, 1)] = pay_out[pl.ds(u, 1)]
    taps_v[144:256] = jnp.zeros((112, TILES * SLOTS), BF16)
    totals[...] = jnp.zeros_like(totals)

    all_but_one(half_in, 0).wait()
    half = half_in[...].astype(F32)
    half = jnp.concatenate([half[:, 0], half[:, 1]], axis=0).astype(BF16)
    mixed = jnp.dot(outer[...], half, preferred_element_type=F32)
    real, imag = mixed[:64], mixed[64:]
    cos_t, sin_t = twist[0], twist[1]
    mixed = jnp.concatenate(
        [real * cos_t + imag * sin_t, imag * cos_t - real * sin_t], axis=1
    ).astype(BF16)
    own = lax.dot_general(
        inner[...], mixed, (((1,), (1,)), ((), ())), preferred_element_type=F32
    )
    own = jnp.concatenate([own[:PIECE], own[256 : 256 + PIECE]], axis=1).astype(BF16)
    grid_all[pl.ds(f, 1)] = own[None]
    pieces = {}
    for dx in (2, 1, 3, 0):
        for dc in (0, 1):
            if dx or dc:
                pieces[dx, dc] = send_near(grid_all.at[f], grid_all, 0, dx, dc)

    all_but_one(pay_in, 1).wait()
    arrived = pay_in[...].astype(F32)
    arrived = jnp.concatenate([arrived[:, 0], arrived[:, 1]], axis=1).T
    for k in range(8):
        fields[k] = jnp.concatenate(
            [arrived[k * 32 + 8 * g : k * 32 + 8 * g + 8] for g in range(4)], axis=1
        )
    table = table_in[...]
    table_high = table.astype(BF16)
    table_low = (table - table_high.astype(F32)).astype(BF16)
    table_both = jnp.concatenate([table_high.astype(F32), table_low.astype(F32)], axis=0).astype(BF16)
    table_narrow = jnp.concatenate([table_high.astype(F32), jnp.zeros((8, 128), F32)], axis=0).astype(BF16)

    def prepare(i, carry):
        lanes = pl.ds(pl.multiple_of(i * BATCH, BATCH), BATCH)
        row, offset_u = fields[2, pl.ds(i, 1), :], fields[3, pl.ds(i, 1), :]
        low, offset_v = fields[5, pl.ds(i, 1), :], fields[6, pl.ds(i, 1), :]
        position = lax.broadcasted_iota(jnp.int32, (128, BATCH), 0).astype(F32)
        hot_u = jnp.where(position == offset_u, 1.0, 0.0).astype(BF16)
        hot_v = jnp.where(position == offset_v, 1.0, 0.0).astype(BF16)
        both = jnp.dot(table_both, hot_u, preferred_element_type=F32)
        factor_u = both[:8] + both[8:]
        factor_v = jnp.dot(table_narrow, hot_v, preferred_element_type=F32)
        away = lax.broadcasted_iota(jnp.int32, (144, BATCH), 0).astype(F32) - low
        across = jnp.zeros((144, BATCH), F32)
        for t in range(TAPS):
            across = jnp.where(away == t, factor_v[t : t + 1], across)
        taps_v[0:144, lanes] = across.astype(BF16)
        across = jnp.concatenate([across, jnp.zeros((112, BATCH), F32)], axis=0)
        taps_t[lanes, :] = across.T.astype(BF16)
        place = lax.broadcasted_iota(jnp.int32, (64, BATCH), 0)
        group = lax.shift_right_logical(place, 3)
        away = (group * OWN + place - group * 8).astype(F32) - row
        down = jnp.zeros((64, BATCH), F32)
        for t in range(TAPS):
            down = jnp.where(away == t, factor_u[t : t + 1], down)
        taps_u[i] = down.reshape(GROUPS, 8, BATCH)
        return carry

    lax.fori_loop(0, batches, prepare, 0, unroll=4)

    for dx in (0, 1, 3, 2):
        there = lax.rem(chip - dx + 4, 4)
        for dc in (0, 1):
            if dx or dc:
                pieces[dx, dc].wait_recv()
        for side in range(2):
            lines = pl.ds(side * PIECE, PIECE)
            piece = grid_all[pl.ds(2 * there + side, 1)].reshape(PIECE, 128)
            windows[there, lines, 0:128] = piece
            piece = piece.astype(F32).reshape(OWN * 2, BLOCKS, 128)
            piece = jnp.concatenate([piece[:, 1:], piece[:, :1]], axis=1)
            windows[there, lines, 128:256] = piece.reshape(PIECE, 128).astype(BF16)

        def sample(i, carry):
            lanes = pl.ds(pl.multiple_of(i * BATCH, BATCH), BATCH)
            sampled = jnp.dot(windows[there], taps_v[:, lanes], preferred_element_type=F32)
            total = totals[i]
            for side in range(2):
                taps = taps_u[i, pl.ds(2 * there + side, 1)].reshape(8, BATCH)
                for r in range(OWN):
                    n = (side * OWN + r) * 32
                    total = total + sampled[n : n + 32] * taps[r : r + 1]
            totals[i] = total
            return carry

        lax.fori_loop(0, batches, sample, 0, unroll=batches)

    def visit(i, carry):
        lanes = pl.ds(pl.multiple_of(i * BATCH, BATCH), BATCH)
        block = fields[4, pl.ds(i, 1), :]
        here = lax.broadcasted_iota(jnp.int32, (BLOCKS, BATCH), 0).astype(F32) == block
        parts = []
        for c in range(2):
            found = jnp.where(here, totals[i, c * BLOCKS : (c + 1) * BLOCKS], 0.0)
            found = jnp.sum(found, axis=0, keepdims=True)
            model[c, pl.ds(i, 1), :] = found
            parts.append(jnp.where(here, fields[c, pl.ds(i, 1), :] - found, 0.0))
        left = jnp.concatenate(parts, axis=0)
        for g in range(GROUPS):
            taps = taps_u[i, g]
            for r in range(OWN):
                n = (g % 2 * OWN + r) * 32
                deposit[g // 2, n : n + 32, lanes] = (left * taps[r : r + 1]).astype(BF16)
        return carry

    lax.fori_loop(0, batches, visit, 0, unroll=batches)

    sums = {}
    for dx in (2, 1, 3, 0):
        there = lax.rem(chip + dx, 4)
        spread = jnp.dot(deposit[there], taps_t[...], preferred_element_type=F32)
        for side in range(2):
            piece = spread[side * PIECE : (side + 1) * PIECE]
            over = piece[:, 128:256].reshape(OWN * 2, BLOCKS, 128)
            over = jnp.concatenate([over[:, BLOCKS - 1 :], over[:, : BLOCKS - 1]], axis=1)
            piece = (piece[:, 0:128] + over.reshape(PIECE, 128)).astype(BF16)
            part_out[pl.ds(2 * there + side, 1)] = piece[None]
        for dc in (0, 1):
            if dx or dc:
                sums[dx, dc] = send_near(part_out.at[at(dx, dc)], part_in, 1, dx, dc)
    part_in[pl.ds(f, 1)] = part_out[pl.ds(f, 1)]

    lines = []
    for c in range(2):
        values = model[c]
        for g in range(4):
            lines.append(values[:, 64 * g : 64 * g + 64])
    lines.append(jnp.zeros((64, 64), F32))
    back_out[...] = jnp.concatenate(lines, axis=0).T.reshape(TILES, 1, 128)
    scatter_uv(back_out, back_in, 2)
    back_in[pl.ds(u, 1)] = back_out[pl.ds(u, 1)]

    for copy in sums.values():
        copy.wait_recv()
    whole = part_in[0].astype(F32)
    for g in range(1, GROUPS):
        whole = whole + part_in[g].astype(F32)

    whole = jnp.concatenate([whole, jnp.zeros((256 - PIECE, 128), F32)], axis=0).T
    whole = jnp.concatenate([whole[:64], whole[64:]], axis=1).astype(BF16)
    mixed = jnp.dot(whole, inner[...], preferred_element_type=F32)
    real, imag = mixed[:, :256], mixed[:, 256:]
    mixed = jnp.concatenate(
        [real * cos_t - imag * sin_t, imag * cos_t + real * sin_t], axis=0
    ).astype(BF16)
    column = jnp.dot(outer_t[...], mixed, preferred_element_type=F32)
    col_out[...] = jnp.stack([column[:TILES], column[TILES:]], axis=1).astype(BF16)
    scatter_uv(col_out, col_in, 3)
    col_in[pl.ds(u, 1)] = col_out[pl.ds(u, 1)]

    all_but_one(back_in, 2).wait()
    sampled = back_in[...].reshape(TILES, 128).T
    for c in range(2):
        residual_ref[c] = jnp.where(
            slot < counts[...], vis[c] - sampled[c * SLOTS : (c + 1) * SLOTS], 0.0
        )
    for copies in (pieces, sums):
        for copy in copies.values():
            copy.wait_send()

    all_but_one(col_in, 3).wait()
    column = col_in[...].astype(F32)
    column = jnp.concatenate([column[:, 0], column[:, 1]], axis=0).T
    column = jnp.concatenate(
        [column[r * STRIP : (r + 1) * STRIP] for r in range(OWN)], axis=1
    ).astype(BF16)
    shares = {}
    for dx in (2, 1, 3, 0):
        there = lax.rem(chip + dx, 4)
        lanes = pl.ds(pl.multiple_of(there * 512, 512), 512)
        dirty = jnp.dot(column, basis[:, lanes], preferred_element_type=F32)
        for side in range(2):
            piece = dirty[:, side * 256 : (side + 1) * 256].astype(BF16)
            dirty_out[pl.ds(2 * there + side, 1)] = piece[None]
        for dc in (0, 1):
            if dx or dc:
                shares[dx, dc] = send_near(dirty_out.at[at(dx, dc)], dirty_in, 2, dx, dc)
    dirty_in[pl.ds(f, 1)] = dirty_out[pl.ds(f, 1)]
    for copy in shares.values():
        copy.wait()
    picture = dirty_in[0].astype(F32)
    for g in range(1, GROUPS):
        picture = picture + dirty_in[g].astype(F32)
    grad_ref[...] = picture


def publish(residual_ref, grad_ref, residual_hbm, grad_hbm, sems):
    copies = [
        pltpu.make_async_copy(residual_ref, residual_hbm, sems.at[0]),
        pltpu.make_async_copy(grad_ref, grad_hbm, sems.at[1]),
    ]
    for copy in copies:
        copy.start()
    for copy in copies:
        copy.wait()


def per_device(
    model_image, visibilities, cell_rows, cell_cols, kernel_offsets, slot_counts, kernel_table
):
    constants = [jnp.asarray(x) for x in tables()]
    inputs = [
        model_image,
        visibilities.reshape(2, TILES, SLOTS).transpose(0, 2, 1),
        cell_rows.reshape(TILES, SLOTS).T,
        cell_cols.reshape(TILES, SLOTS).T,
        kernel_offsets.reshape(2, TILES, SLOTS).transpose(0, 2, 1),
        slot_counts.reshape(1, TILES),
        kernel_table.T,
    ] + constants
    vmem = pl.BlockSpec(memory_space=pltpu.VMEM)
    hbm = pl.BlockSpec(memory_space=pltpu.HBM)
    batches = TILES * SLOTS // BATCH
    local = [pltpu.VMEM(x.shape[1:] if n == 8 else x.shape, x.dtype) for n, x in enumerate(inputs)]
    residual, gradient = pl.pallas_call(
        kernel,
        out_shape=(
            pltpu.VMEM((2, SLOTS, TILES), F32),
            pltpu.VMEM((STRIP, WIDTH // GROUPS), F32),
        ),
        in_specs=[hbm] * len(inputs),
        out_specs=(vmem, vmem),
        scratch_shapes=local
        + [
            pltpu.VMEM((OWN * 128, WIDTH), BF16),
            pltpu.VMEM((TILES, 2, 256), BF16),
            pltpu.VMEM((TILES, 2, 256), BF16),
            pltpu.VMEM((TILES, 2, 128), BF16),
            pltpu.VMEM((TILES, 2, 128), BF16),
            pltpu.VMEM((8, batches, BATCH), F32),
            pltpu.VMEM((GROUPS, PIECE, 128), BF16),
            pltpu.VMEM((4, 2 * PIECE, 256), BF16),
            pltpu.VMEM((256, TILES * SLOTS), BF16),
            pltpu.VMEM((TILES * SLOTS, 256), BF16),
            pltpu.VMEM((batches, GROUPS, 8, BATCH), F32),
            pltpu.VMEM((batches, 2 * BLOCKS, BATCH), F32),
            pltpu.VMEM((4, 2 * PIECE, TILES * SLOTS), BF16),
            pltpu.VMEM((2, batches, BATCH), F32),
            pltpu.VMEM((TILES, 1, 128), F32),
            pltpu.VMEM((TILES, 1, 128), F32),
            pltpu.VMEM((GROUPS, PIECE, 128), BF16),
            pltpu.VMEM((GROUPS, PIECE, 128), BF16),
            pltpu.VMEM((TILES, 2, 256), BF16),
            pltpu.VMEM((TILES, 2, 256), BF16),
            pltpu.VMEM((GROUPS, STRIP, WIDTH // GROUPS), BF16),
            pltpu.VMEM((GROUPS, STRIP, WIDTH // GROUPS), BF16),
            pltpu.SemaphoreType.DMA((len(inputs),)),
            pltpu.SemaphoreType.DMA((4,)),
            pltpu.SemaphoreType.DMA((4,)),
            pltpu.SemaphoreType.DMA((3, GROUPS)),
            pltpu.SemaphoreType.DMA((3, GROUPS)),
        ],
        compiler_params=pltpu.CompilerParams(
            collective_id=0, has_side_effects=True, vmem_limit_bytes=40 << 20
        ),
    )(*[pltpu.with_memory_space_constraint(x, pltpu.HBM) for x in inputs])
    residual, gradient = pl.pallas_call(
        publish,
        out_shape=(
            jax.ShapeDtypeStruct((2, SLOTS, TILES), F32),
            jax.ShapeDtypeStruct((STRIP, WIDTH // GROUPS), F32),
        ),
        in_specs=[vmem] * 2,
        out_specs=(hbm, hbm),
        scratch_shapes=[pltpu.SemaphoreType.DMA((2,))],
        compiler_params=pltpu.CompilerParams(vmem_limit_bytes=1 << 20),
    )(residual, gradient)
    return residual.transpose(0, 2, 1).reshape(2, 1, 1, TILES, SLOTS), gradient


def solution(mesh):
    placed = (
        P("uv", None),
        P(None, "uv", "freq", None, None),
        P("uv", "freq", None, None),
        P("uv", "freq", None, None),
        P(None, "uv", "freq", None, None),
        P("uv", "freq", None),
        P(),
    )
    return jax.shard_map(
        per_device,
        mesh=mesh,
        in_specs=placed,
        out_specs=(P(None, "uv", "freq", None, None), P("uv", "freq")),
        check_vma=False,
    )
```
